32 devices in a mesh: mkt: 8 (over z, y), draw: 4 (over x, core).
Axes of the slice: x: 2, y: 2, z: 4, core: 2. Of those that a mesh axis runs over, the one named last changes fastest.
Arguments:
- x_char: float32 [384, 56, 8], P('mkt'), may hold values from -2.5 to 2.5
- nu_draws: float32 [384, 8, 2048], P('mkt', None, 'draw'), may hold values from -3 to 3
- coef_sigma: float32 [8], replicated, may hold values from 0.3 to 1.2
- log_share: float32 [384, 56], P('mkt'), may hold values from -7 to -4.5
- counts: int32 [384], P('mkt'), may hold values from 28 to 56
Outputs:
- mean_util: float32 [384, 56], P('mkt')
- jacobian: float32 [384, 56, 56], P(('mkt', 'draw'))
- sup_norms: float32 [3], replicated
The draws below stay inside these ranges and needn't reach their ends.
Inputs may be any that keep to these rules, and one draw needn't show every extreme that they name: Products 0 to counts - 1 of a market are valid; the other slots are padding.
All inputs are finite; a program needn't handle non-finite values. Where the reference program divides by a largest or mean magnitude, that divisor is 1e-20 or more.
Results may differ from the reference program's by a relative error of at most 0.00013.
Values sent between devices are 32-bit elements; how exact they have to be, the bound alone decides.
A program may use at most 64 MiB of HBM per device.

```python
import math
import jax
import jax.numpy as jnp
from jax import lax

J = 56
K = 8
ITERS = 3
M = 384
R = 2048


def set_ends(array, key, least, top_value):
    longest = array.shape.index(max(array.shape))
    spots = []
    for shift in (0, 1):
        where = [jax.random.randint(jax.random.fold_in(key, axis), (), 0, length) for axis, length in enumerate(array.shape)]
        where[longest] = (where[longest] + shift) % array.shape[longest]
        spots.append(tuple(where))
    return array.at[spots[0]].set(least).at[spots[1]].set(top_value)


def shard_levels(key, shape, pieces, least, top_value):
    gain, own = 1.0, jax.random.fold_in(key, 6)
    for position, blocks in pieces:
        heights = jnp.exp(jax.random.uniform(jax.random.fold_in(own, position), (blocks,), jnp.float32, least / len(pieces), top_value / len(pieces)))
        gain = gain * jnp.repeat(heights, shape[position] // blocks).reshape([-1 if axis == position else 1 for axis in range(len(shape))])
    return gain


def gaussian(key, shape, spread, bound, cuts=(), kind=jnp.bfloat16):
    array = spread * jax.random.normal(key, shape, jnp.float32)
    if cuts:
        array = array * shard_levels(key, shape, cuts, -0.22, 0.18)
    return jnp.clip(array, -bound, bound).astype(kind)


def setup_inputs(seed: int = 0) -> dict:
    seeds = jax.random.split(jax.random.key(seed), 6)
    return {
        "x_char": gaussian(seeds[0], (M, J, K), 1.0, 2.5, ((0, 8),), jnp.float32),
        "nu_draws": gaussian(seeds[1], (M, K, R), 1.0, 3.0, ((0, 8), (2, 4)), jnp.float32),
        "coef_sigma": jnp.clip(jnp.exp(jax.random.uniform(seeds[2], (K,), jnp.float32, math.log(0.3), math.log(1.2))), 0.3, 1.2),
        "log_share": jnp.clip(-7.0 + 2.5 * jax.random.uniform(seeds[3], (M, J), jnp.float32) ** shard_levels(seeds[3], (M, J), ((0, 8),), -0.2, 0.2), -7.0, -4.5),
        "counts": set_ends(jax.random.randint(seeds[4], (M,), J // 2, J + 1), jax.random.fold_in(seeds[4], 1), J // 2, J).astype(jnp.int32),
    }


step_cap = 0.25
epsilon = 1e-6


def market_terms(mean_util, scaled, nu_draws, usable, inverse, with_products):
    tastes = jnp.einsum("mjk,mkr->mjr", scaled, nu_draws, precision=lax.Precision.HIGHEST)
    raised = jnp.where(usable[:, :, None], jnp.exp(mean_util[:, :, None] + tastes), 0.0)
    chance = raised / (1.0 + jnp.sum(raised, axis=1, keepdims=True))
    shares = jnp.sum(chance, axis=2) * inverse
    if with_products:
        cross_sums = jnp.einsum("mjr,mlr->mjl", chance, chance, precision=lax.Precision.HIGHEST) * inverse
        return shares, cross_sums
    return shares


def evaluate(mean_util, scaled, nu_draws, usable, inverse, with_products):
    groups = mean_util.shape[0] // 8
    folded = (mean_util.reshape(groups, 8, mean_util.shape[1]),
              scaled.reshape(groups, 8, scaled.shape[1], scaled.shape[2]),
              nu_draws.reshape(groups, 8, nu_draws.shape[1], nu_draws.shape[2]),
              usable.reshape(groups, 8, usable.shape[1]))

    def per_group(items):
        return market_terms(items[0], items[1], items[2], items[3], inverse, with_products)

    def unfold(member):
        return member.reshape((groups * 8,) + member.shape[2:])

    return jax.tree.map(unfold, lax.map(per_group, folded))


def reference(x_char, nu_draws, coef_sigma, log_share, counts):
    usable = jnp.arange(J, dtype=jnp.int32)[None, :] < counts[:, None]
    scaled = x_char * coef_sigma[None, None, :]
    inverse = 1.0 / R
    inside = jnp.sum(jnp.where(usable, jnp.exp(log_share), 0.0), axis=1)
    mean_util = jnp.where(usable, log_share - jnp.log(1.0 - inside)[:, None], 0.0)
    norms_list = []
    for sweep in range(ITERS):
        shares = evaluate(mean_util, scaled, nu_draws, usable, inverse, False)
        change = jnp.where(usable, log_share - jnp.log(jnp.where(usable, shares, 1.0)), 0.0)
        largest = jnp.max(jnp.abs(change))
        mean_util = mean_util + jnp.minimum(1.0, step_cap / (largest + epsilon)) * change
        norms_list.append(largest)
    shares, cross_sums = evaluate(mean_util, scaled, nu_draws, usable, inverse, True)
    divisor = jnp.where(usable, shares, 1.0)
    identity = jnp.eye(J, dtype=jnp.float32)
    paired = usable[:, :, None] & usable[:, None, :]
    jacobian = jnp.where(paired, identity[None, :, :] - cross_sums / divisor[:, :, None], 0.0)
    return mean_util, jacobian, jnp.stack(norms_list)
```

```python
import functools
import math

import jax
import jax.numpy as jnp
from jax import lax
from jax.experimental import pallas as pl
from jax.experimental.pallas import tpu as pltpu
from jax.sharding import PartitionSpec as P

ITERS = 3
LANES = 128
MESH = pl.DeviceIdType.MESH

step_cap = 0.25
epsilon = 1e-06


def divisor_up_to(count, most):
    return max(size for size in range(1, most + 1) if count % size == 0)


def rounded(value):
    return value.astype(jnp.bfloat16).astype(jnp.float32)


def split3(value):
    first = rounded(value)
    second = rounded(value - first)
    return first, second, (value - first) - second


def kernel(
    draws,
    chips,
    inverse,
    sigma_ref,
    counts_ref,
    counts_row_ref,
    log_share_ref,
    x_ref,
    nu_ref,
    mean_out,
    jac_out,
    norms_out,
    held,
    square,
    part_slots,
    peak_slots,
    cross_send,
    cross_slots,
    part_send_sem,
    part_recv_sem,
    peak_send_sem,
    peak_recv_sem,
    cross_send_sem,
    cross_recv_sem,
):
    markets, coefs, slots = x_ref.shape
    own = markets // draws
    half = LANES // 2 if slots + 8 <= LANES // 2 else LANES
    pack = LANES // half
    group = divisor_up_to(markets, 8)
    my_draw = lax.axis_index("draw")
    my_mkt = lax.axis_index("mkt")

    barrier = pltpu.get_barrier_semaphore()
    for k in range(1, draws):
        pl.semaphore_signal(
            barrier, inc=1, device_id={"draw": lax.rem(my_draw + k, draws)}, device_id_type=MESH
        )
    for k in range(1, chips):
        pl.semaphore_signal(
            barrier, inc=1, device_id={"mkt": lax.rem(my_mkt + k, chips)}, device_id_type=MESH
        )

    lane = lax.broadcasted_iota(jnp.int32, (slots, LANES), 1)
    row = lax.broadcasted_iota(jnp.int32, (slots, LANES), 0)

    square[...] = jnp.zeros_like(square)
    square[0:markets, 0:slots] = log_share_ref[...]
    log_share = square[...].T[0:slots, :]
    square[0:1, 0:markets] = counts_row_ref[...].astype(jnp.float32)
    counts = square[0:1, :]
    usable = (row.astype(jnp.float32) < counts) & (lane < markets)
    inside = jnp.sum(jnp.where(usable, jnp.exp(log_share), 0.0), axis=0, keepdims=True)
    mean = jnp.where(usable, log_share - jnp.log(1.0 - inside), 0.0)

    coef_row = lax.broadcasted_iota(jnp.int32, (coefs, slots), 0)
    sigma = jnp.zeros((coefs, slots), jnp.float32)
    for k in range(coefs):
        sigma = jnp.where(coef_row == k, sigma_ref[k], sigma)

    def raised_tastes(m):
        s1, s2, s3 = split3(x_ref[m] * sigma * math.log2(math.e))
        n1, n2, n3 = split3(nu_ref[m])
        left = jnp.concatenate([s1, s1, s2, s2, s1, s3], axis=0).astype(jnp.bfloat16)
        right = jnp.concatenate([n1, n2, n1, n2, n3, n1], axis=0).astype(jnp.bfloat16)
        tastes = lax.dot_general(
            left, right, (((0,), (0,)), ((), ())), preferred_element_type=jnp.float32
        )
        return jnp.exp2(tastes)

    def sweep(weights, first):
        def body(g, total):
            base = g * group
            local = pltpu.roll(weights, lax.rem(LANES - base, LANES), 1)
            part = jnp.zeros((slots, LANES), jnp.float32)
            for i in range(group):
                if first:
                    e = raised_tastes(base + i)
                    held[base + i] = e
                else:
                    e = held[base + i]
                denominator = 1.0 + jnp.sum(local[:, i : i + 1] * e, axis=0, keepdims=True)
                column = jnp.sum(e * (1.0 / denominator), axis=1, keepdims=True)
                part = jnp.where(lane == i, column, part)
            return total + pltpu.roll(part, base, 1)

        return lax.fori_loop(0, markets // group, body, jnp.zeros((slots, LANES), jnp.float32))

    def part_copy(it, k):
        return pltpu.make_async_remote_copy(
            src_ref=part_slots.at[it, my_draw],
            dst_ref=part_slots.at[it, my_draw],
            send_sem=part_send_sem.at[it, k - 1],
            recv_sem=part_recv_sem.at[it, k - 1],
            device_id={"draw": lax.rem(my_draw + k, draws)},
            device_id_type=MESH,
        )

    def peak_copy(it, k):
        return pltpu.make_async_remote_copy(
            src_ref=peak_slots.at[it, 0],
            dst_ref=peak_slots.at[it, k],
            send_sem=peak_send_sem.at[it, k - 1],
            recv_sem=peak_recv_sem.at[it, k - 1],
            device_id={"mkt": lax.rem(my_mkt + k, chips)},
            device_id_type=MESH,
        )

    for it in range(ITERS):
        weights = jnp.where(usable, jnp.exp(mean), 0.0)
        partial_value = sweep(weights, it == 0)
        part_slots[it, my_draw] = partial_value
        if it == 0:
            pl.semaphore_wait(barrier, draws - 1 + chips - 1)
        for k in range(1, draws):
            part_copy(it, k).start()
        for k in range(1, draws):
            part_copy(it, k).wait()
        total = part_slots[it, 0]
        for d in range(1, draws):
            total = total + part_slots[it, d]
        shares = weights * total * inverse
        change = jnp.where(usable, log_share - jnp.log(jnp.where(usable, shares, 1.0)), 0.0)
        peak = jnp.max(jnp.abs(change), axis=0, keepdims=True)
        peak = jnp.max(peak, axis=1, keepdims=True)
        peak_slots[it, 0] = jnp.broadcast_to(peak, (8, LANES))
        for k in range(1, chips):
            peak_copy(it, k).start()
        for k in range(1, chips):
            peak_copy(it, k).wait()
        largest = peak_slots[it, 0]
        for k in range(1, chips):
            largest = jnp.maximum(largest, peak_slots[it, k])
        norms_out[it] = largest[0, 0]
        largest = largest[0:1, :]
        mean = mean + jnp.minimum(1.0, step_cap / (largest + epsilon)) * change

    weights = jnp.where(usable, jnp.exp(mean), 0.0)
    ones = jnp.ones((8, nu_ref.shape[2]), jnp.float32)
    doubled = jnp.where(
        lax.broadcasted_iota(jnp.int32, (slots, slots + 8), 1) < slots, 2.0, 1.0
    )

    def cross_copy(k):
        return pltpu.make_async_remote_copy(
            src_ref=cross_send.at[k - 1],
            dst_ref=cross_slots.at[k - 1],
            send_sem=cross_send_sem.at[k - 1],
            recv_sem=cross_recv_sem.at[k - 1],
            device_id={"draw": lax.rem(my_draw + k, draws)},
            device_id_type=MESH,
        )

    def last_sweep(k, carry):
        base = lax.rem(my_draw + k, draws) * own
        local = pltpu.roll(weights, lax.rem(LANES - base, LANES), 1)
        for i in range(own):
            e = held[base + i]
            raised = local[:, i : i + 1] * e
            denominator = 1.0 + jnp.sum(raised, axis=0, keepdims=True)
            chance = raised * (1.0 / denominator)
            both = jnp.concatenate([chance, chance - rounded(chance)], axis=0)
            right = jnp.concatenate([chance, ones], axis=0).astype(jnp.bfloat16)
            products = lax.dot_general(
                both.astype(jnp.bfloat16),
                right,
                (((1,), (1,)), ((), ())),
                preferred_element_type=jnp.float32,
            )
            merged = products[0:slots] + products[slots:] * doubled
            at = (i % pack) * half
            cross_send[k - 1, i // pack, :, at : at + slots + 8] = merged

        @pl.when(k < draws)
        def _():
            cross_copy(k).start()

        return carry

    lax.fori_loop(1, draws + 1, last_sweep, 0)

    square[0:slots, :] = mean
    mean_out[...] = square[...].T[0:markets, 0:slots]

    for k in range(1, draws):
        cross_copy(k).wait()

    eye = (row == lane)[:, 0:slots]
    for pair in range(cross_send.shape[1]):
        total = cross_send[draws - 1, pair]
        for k in range(1, draws):
            total = total + cross_slots[k - 1, pair]
        for i in range(pack):
            if pair * pack + i >= own:
                continue
            wide = total if i == 0 else pltpu.roll(total, LANES - i * half, 1)
            square[0:slots, :] = wide
            turned = square[...].T[0:slots, 0:slots]
            cross = 0.5 * (wide[:, 0:slots] + turned)
            count = counts_ref[my_draw * own + pair * pack + i]
            here = row < count
            divisor = jnp.where(here, wide, 1.0)[:, slots : slots + 1]
            jac_out[pair * pack + i] = jnp.where(
                (here & (lane < count))[:, 0:slots],
                jnp.where(eye, 1.0, 0.0) - cross / divisor,
                0.0,
            )


def shards(x_char, nu_draws, coef_sigma, log_share, counts):
    markets, slots, coefs = x_char.shape
    consumers = nu_draws.shape[2]
    draws, chips = lax.axis_size("draw"), lax.axis_size("mkt")
    own = markets // draws
    half = LANES // 2 if slots + 8 <= LANES // 2 else LANES
    blocks = -(-own // (LANES // half))
    vmem = pl.BlockSpec(memory_space=pltpu.VMEM)
    smem = pl.BlockSpec(memory_space=pltpu.SMEM)
    f32 = jnp.float32
    return pl.pallas_call(
        functools.partial(kernel, draws, chips, 1.0 / (consumers * draws)),
        out_shape=(
            jax.ShapeDtypeStruct((markets, slots), f32),
            jax.ShapeDtypeStruct((own, slots, slots), f32),
            jax.ShapeDtypeStruct((ITERS,), f32),
        ),
        in_specs=[smem, smem, vmem, vmem, vmem, vmem],
        out_specs=(vmem, vmem, smem),
        scratch_shapes=[
            pltpu.VMEM((markets, slots, consumers), f32),
            pltpu.VMEM((LANES, LANES), f32),
            pltpu.VMEM((ITERS, draws, slots, LANES), f32),
            pltpu.VMEM((ITERS, chips, 8, LANES), f32),
            pltpu.VMEM((draws, blocks, slots, LANES), f32),
            pltpu.VMEM((draws, blocks, slots, LANES), f32),
            pltpu.SemaphoreType.DMA((ITERS, draws)),
            pltpu.SemaphoreType.DMA((ITERS, draws)),
            pltpu.SemaphoreType.DMA((ITERS, chips)),
            pltpu.SemaphoreType.DMA((ITERS, chips)),
            pltpu.SemaphoreType.DMA((draws,)),
            pltpu.SemaphoreType.DMA((draws,)),
        ],
        compiler_params=pltpu.CompilerParams(
            collective_id=0, has_side_effects=True, vmem_limit_bytes=48 * 1024 * 1024
        ),
        name="contraction",
    )(
        coef_sigma,
        counts,
        counts[None, :],
        log_share,
        jnp.swapaxes(x_char, 1, 2),
        nu_draws,
    )


def solution(mesh):
    return jax.shard_map(
        shards,
        mesh=mesh,
        in_specs=(P("mkt", None, None), P("mkt", None, "draw"), P(), P("mkt", None), P("mkt")),
        out_specs=(P("mkt", None), P(("mkt", "draw"), None, None), P()),
        check_vma=False,
    )
```

```python
import functools
import math

import jax
import jax.numpy as jnp
from jax import lax
from jax.experimental import pallas as pl
from jax.experimental.pallas import tpu as pltpu
from jax.sharding import PartitionSpec as P

ITERS = 3
LANES = 128
GROUP = 16
VMEM_LIMIT = 66_500_000
MESH = pl.DeviceIdType.MESH

step_cap = 0.25
epsilon = 1e-06


def divisor_up_to(count, most):
    return max(size for size in range(1, most + 1) if count % size == 0)


def rounded(value):
    return value.astype(jnp.bfloat16).astype(jnp.float32)


def split2(value):
    first = rounded(value)
    return first, value - first


def kernel(
    draws,
    chips,
    inverse,
    sigma_hbm,
    counts_hbm,
    counts_row_hbm,
    log_share_hbm,
    x_hbm,
    nu_hbm,
    mean_out,
    jac_out,
    norms_out,
    sigma_ref,
    counts_ref,
    counts_row_ref,
    log_share_ref,
    x_ref,
    nu_ref,
    held,
    inverse_ref,
    square,
    part_slots,
    peak_slots,
    cross_send,
    cross_slots,
    part_send_sem,
    part_recv_sem,
    peak_send_sem,
    peak_recv_sem,
    cross_send_sem,
    cross_recv_sem,
    load_sem,
    nu_sem,
):
    markets, coefs, slots = x_ref.shape
    own = markets // draws
    half = LANES // 2 if slots + 8 <= LANES // 2 else LANES
    pack = LANES // half
    group = divisor_up_to(markets, GROUP)
    folds = part_slots.shape[2]
    my_draw = lax.axis_index("draw")
    my_mkt = lax.axis_index("mkt")

    loads = [
        pltpu.make_async_copy(source, target, load_sem.at[n])
        for n, (source, target) in enumerate(
            (
                (counts_row_hbm, counts_row_ref),
                (log_share_hbm, log_share_ref),
                (sigma_hbm, sigma_ref),
                (counts_hbm, counts_ref),
                (x_hbm, x_ref),
            )
        )
    ]

    def nu_load(g):
        span = pl.ds(g * group, group)
        return pltpu.make_async_copy(nu_hbm.at[span], nu_ref.at[span], nu_sem.at[g])

    for load in loads:
        load.start()
    for g in range(markets // group):
        nu_load(g).start()

    barrier = pltpu.get_barrier_semaphore()
    for k in range(1, draws):
        pl.semaphore_signal(
            barrier, inc=1, device_id={"draw": lax.rem(my_draw + k, draws)}, device_id_type=MESH
        )
    for k in range(1, chips):
        pl.semaphore_signal(
            barrier, inc=1, device_id={"mkt": lax.rem(my_mkt + k, chips)}, device_id_type=MESH
        )

    lane = lax.broadcasted_iota(jnp.int32, (slots, LANES), 1)
    row = lax.broadcasted_iota(jnp.int32, (slots, LANES), 0)

    square[...] = jnp.zeros_like(square)
    for load in loads:
        load.wait()
    square[0:markets, 0:slots] = log_share_ref[...]
    log_share = square[...].T[0:slots, :]
    square[0:1, 0:markets] = counts_row_ref[...].astype(jnp.float32)
    counts = square[0:1, :]
    usable = (row.astype(jnp.float32) < counts) & (lane < markets)
    inside = jnp.sum(jnp.where(usable, jnp.exp(log_share), 0.0), axis=0, keepdims=True)
    mean = jnp.where(usable, log_share - jnp.log(1.0 - inside), 0.0)

    coef_row = lax.broadcasted_iota(jnp.int32, (coefs, slots), 0)
    sigma = jnp.zeros((coefs, slots), jnp.float32)
    for k in range(coefs):
        sigma = jnp.where(coef_row == k, sigma_ref[k] * math.log2(math.e), sigma)

    def raised_tastes(m):
        s1, s2 = split2(x_ref[m] * sigma)
        n1, n2 = split2(nu_ref[m])
        left = jnp.concatenate([s1, s1, s2, s2], axis=0).astype(jnp.bfloat16)
        right = jnp.concatenate([n1, n2, n1, n2], axis=0).astype(jnp.bfloat16)
        tastes = lax.dot_general(
            left, right, (((0,), (0,)), ((), ())), preferred_element_type=jnp.float32
        )
        return jnp.exp2(tastes)

    chunks = [
        slice(at, min(at + LANES, nu_ref.shape[2])) for at in range(0, nu_ref.shape[2], LANES)
    ]

    def denominators(weight, m, i, known):
        for chunk in chunks:
            e = held[m, :, chunk] if known is None else known[:, chunk]
            inverse_ref[i : i + 1, chunk] = 1.0 + jnp.sum(weight * e, axis=0, keepdims=True)

    def sweep(weights, first):
        def body(g, total):
            base = g * group
            if first:
                nu_load(g).wait()
            local = pltpu.roll(weights, lax.rem(LANES - base, LANES), 1)
            for i in range(group):
                known = None
                if first:
                    known = raised_tastes(base + i)
                    held[base + i] = known
                denominators(local[:, i : i + 1], base + i, i, known)
            inverse_ref[0:group] = 1.0 / inverse_ref[0:group]
            part = jnp.zeros((slots, LANES), jnp.float32)
            for i in range(group):
                column = None
                for chunk in chunks:
                    term = held[base + i, :, chunk] * inverse_ref[i : i + 1, chunk]
                    column = term if column is None else column + term
                part = jnp.where(lane == i, jnp.sum(column, axis=1, keepdims=True), part)
            return total + pltpu.roll(part, base, 1)

        return lax.fori_loop(0, markets // group, body, jnp.zeros((slots, LANES), jnp.float32))

    def fold(value):
        if folds == slots:
            return value
        low = jnp.concatenate(
            [value[folds:], jnp.zeros((2 * folds - slots, LANES), jnp.float32)], axis=0
        )
        return value[0:folds] + pltpu.roll(low, LANES // 2, 1)

    def unfold(value):
        if folds == slots:
            return value
        return jnp.concatenate(
            [value, pltpu.roll(value, LANES // 2, 1)[0 : slots - folds]], axis=0
        )

    def part_copy(it, k):
        return pltpu.make_async_remote_copy(
            src_ref=part_slots.at[it, my_draw],
            dst_ref=part_slots.at[it, my_draw],
            send_sem=part_send_sem.at[it, k - 1],
            recv_sem=part_recv_sem.at[it, k - 1],
            device_id={"draw": lax.rem(my_draw + k, draws)},
            device_id_type=MESH,
        )

    def peak_copy(it, k):
        return pltpu.make_async_remote_copy(
            src_ref=peak_slots.at[it, 0],
            dst_ref=peak_slots.at[it, k],
            send_sem=peak_send_sem.at[it, k - 1],
            recv_sem=peak_recv_sem.at[it, k - 1],
            device_id={"mkt": lax.rem(my_mkt + k, chips)},
            device_id_type=MESH,
        )

    norms = []
    for it in range(ITERS):
        weights = jnp.where(usable, jnp.exp(mean), 0.0)
        partial_value = sweep(weights, it == 0)
        part_slots[it, my_draw] = fold(partial_value)
        if it == 0:
            pl.semaphore_wait(barrier, draws - 1 + chips - 1)
        for k in range(1, draws):
            part_copy(it, k).start()
        for k in range(1, draws):
            part_copy(it, k).wait()
        total = part_slots[it, 0]
        for d in range(1, draws):
            total = total + part_slots[it, d]
        shares = weights * unfold(total) * inverse
        change = jnp.where(usable, log_share - jnp.log(jnp.where(usable, shares, 1.0)), 0.0)
        peak = jnp.max(jnp.abs(change), axis=0, keepdims=True)
        peak = jnp.max(peak, axis=1, keepdims=True)
        peak_slots[it, 0] = jnp.broadcast_to(peak, (1, LANES))
        for k in range(1, chips):
            peak_copy(it, k).start()
        for k in range(1, chips):
            peak_copy(it, k).wait()
        largest = peak_slots[it, 0]
        for k in range(1, chips):
            largest = jnp.maximum(largest, peak_slots[it, k])
        norms.append(largest)
        mean = mean + jnp.minimum(1.0, step_cap / (largest + epsilon)) * change

    weights = jnp.where(usable, jnp.exp(mean), 0.0)
    ones = jnp.ones((8, nu_ref.shape[2]), jnp.float32)
    doubled = jnp.where(
        lax.broadcasted_iota(jnp.int32, (slots, slots + 8), 1) < slots, 2.0, 1.0
    )

    cores = 2 if draws % 2 == 0 else 1

    def partner(k):
        chip = (my_draw // cores + (k - 1) // cores + 1) % (draws // cores)
        core = (my_draw + k) % cores
        return chip * cores + core

    def cross_copy(k):
        return pltpu.make_async_remote_copy(
            src_ref=cross_send.at[k - 1],
            dst_ref=cross_slots.at[k - 1],
            send_sem=cross_send_sem.at[k - 1],
            recv_sem=cross_recv_sem.at[k - 1],
            device_id={"draw": partner(k)},
            device_id_type=MESH,
        )

    def last_sweep(k, carry):
        base = partner(k) * own
        local = pltpu.roll(weights, lax.rem(LANES - base, LANES), 1)
        for i in range(own):
            raised = local[:, i : i + 1] * held[base + i]
            denominator = 1.0 + jnp.sum(raised, axis=0, keepdims=True)
            chance = raised * (1.0 / denominator)
            both = jnp.concatenate([chance, chance - rounded(chance)], axis=0)
            right = jnp.concatenate([chance, ones], axis=0).astype(jnp.bfloat16)
            products = lax.dot_general(
                both.astype(jnp.bfloat16),
                right,
                (((1,), (1,)), ((), ())),
                preferred_element_type=jnp.float32,
            )
            merged = products[0:slots] + products[slots:] * doubled
            at = (i % pack) * half
            cross_send[k - 1, i // pack, :, at : at + slots + 8] = merged

        @pl.when(k < draws)
        def _():
            cross_copy(k).start()

        return carry

    lax.fori_loop(1, draws + 1, last_sweep, 0)

    square[0:slots, :] = mean
    mean_out[...] = square[...].T[0:markets, 0:slots]
    for it in range(ITERS):
        norms_out[it] = norms[it][0, 0]

    for k in range(1, draws):
        cross_copy(k).wait()

    eye = jnp.where(row == lane, 1.0, 0.0)
    for pair in range(cross_send.shape[1]):
        total = cross_send[draws - 1, pair]
        for k in range(1, draws):
            total = total + cross_slots[k - 1, pair]
        square[0:slots, :] = total
        turned = square[...].T
        for i in range(pack):
            if pair * pack + i >= own:
                continue
            wide = total if i == 0 else pltpu.roll(total, LANES - i * half, 1)
            cross = 0.5 * (wide[:, 0:slots] + turned[i * half : i * half + slots, 0:slots])
            count = counts_ref[my_draw * own + pair * pack + i]
            here = row < count
            divisor = jnp.where(here, wide, 1.0)[:, slots : slots + 1]
            jac_out[pair * pack + i] = jnp.where(
                (here & (lane < count))[:, 0:slots],
                eye[:, 0:slots] - cross / divisor,
                0.0,
            )


def shards(x_char, nu_draws, coef_sigma, log_share, counts):
    markets, slots, coefs = x_char.shape
    consumers = nu_draws.shape[2]
    draws, chips = lax.axis_size("draw"), lax.axis_size("mkt")
    own = markets // draws
    half = LANES // 2 if slots + 8 <= LANES // 2 else LANES
    folds = -(-slots // 16) * 8 if markets <= LANES // 2 else slots
    blocks = -(-own // (LANES // half))
    vmem = pl.BlockSpec(memory_space=pltpu.VMEM)
    smem = pl.BlockSpec(memory_space=pltpu.SMEM)
    f32 = jnp.float32
    return pl.pallas_call(
        functools.partial(kernel, draws, chips, 1.0 / (consumers * draws)),
        out_shape=(
            jax.ShapeDtypeStruct((markets, slots), f32),
            jax.ShapeDtypeStruct((own, slots, slots), f32),
            jax.ShapeDtypeStruct((ITERS,), f32),
        ),
        in_specs=[pl.BlockSpec(memory_space=pltpu.HBM)] * 6,
        out_specs=(vmem, vmem, smem),
        scratch_shapes=[
            pltpu.SMEM((coefs,), f32),
            pltpu.SMEM((markets,), jnp.int32),
            pltpu.VMEM((1, markets), jnp.int32),
            pltpu.VMEM((markets, slots), f32),
            pltpu.VMEM((markets, coefs, slots), f32),
            pltpu.VMEM((markets, coefs, consumers), f32),
            pltpu.VMEM((markets, slots, consumers), f32),
            pltpu.VMEM((divisor_up_to(markets, GROUP), consumers), f32),
            pltpu.VMEM((LANES, LANES), f32),
            pltpu.VMEM((ITERS, draws, folds, LANES), f32),
            pltpu.VMEM((ITERS, chips, 1, LANES), f32),
            pltpu.VMEM((draws, blocks, slots, LANES), f32),
            pltpu.VMEM((draws, blocks, slots, LANES), f32),
            pltpu.SemaphoreType.DMA((ITERS, draws)),
            pltpu.SemaphoreType.DMA((ITERS, draws)),
            pltpu.SemaphoreType.DMA((ITERS, chips)),
            pltpu.SemaphoreType.DMA((ITERS, chips)),
            pltpu.SemaphoreType.DMA((draws,)),
            pltpu.SemaphoreType.DMA((draws,)),
            pltpu.SemaphoreType.DMA((5,)),
            pltpu.SemaphoreType.DMA((markets // divisor_up_to(markets, GROUP),)),
        ],
        compiler_params=pltpu.CompilerParams(
            collective_id=0, has_side_effects=True, vmem_limit_bytes=VMEM_LIMIT
        ),
        name="contraction",
    )(
        coef_sigma,
        counts,
        counts[None, :],
        log_share,
        jnp.swapaxes(x_char, 1, 2),
        nu_draws,
    )


def solution(mesh):
    return jax.shard_map(
        shards,
        mesh=mesh,
        in_specs=(P("mkt", None, None), P("mkt", None, "draw"), P(), P("mkt", None), P("mkt")),
        out_specs=(P("mkt", None), P(("mkt", "draw"), None, None), P()),
        check_vma=False,
    )
```

```python
import functools
import math

import jax
import jax.numpy as jnp
from jax import lax
from jax.experimental import pallas as pl
from jax.experimental.pallas import tpu as pltpu
from jax.sharding import PartitionSpec as P

ITERS = 3
LANES = 128
GROUP = 16
VMEM_LIMIT = 66_500_000
MESH = pl.DeviceIdType.MESH

step_cap = 0.25
epsilon = 1e-06


def divisor_up_to(count, most):
    return max(size for size in range(1, most + 1) if count % size == 0)


def rounded(value):
    return value.astype(jnp.bfloat16).astype(jnp.float32)


def split2(value):
    first = rounded(value)
    return first, value - first


def kernel(
    draws,
    chips,
    inverse,
    sigma_hbm,
    counts_hbm,
    counts_row_hbm,
    log_share_hbm,
    x_hbm,
    nu_hbm,
    mean_out,
    jac_out,
    norms_out,
    sigma_ref,
    counts_ref,
    counts_row_ref,
    log_share_ref,
    x_ref,
    nu_ref,
    held,
    inverse_ref,
    weights_ref,
    turned_ref,
    square,
    part_slots,
    peak_slots,
    cross_send,
    cross_slots,
    part_send_sem,
    part_recv_sem,
    peak_send_sem,
    peak_recv_sem,
    cross_send_sem,
    cross_recv_sem,
    load_sem,
    nu_sem,
):
    markets, coefs, slots = x_ref.shape
    own = markets // draws
    half = LANES // 2
    tiles = slots // 8
    group = divisor_up_to(markets, min(GROUP, LANES // tiles))
    groups = markets // group
    my_draw = lax.axis_index("draw")
    my_mkt = lax.axis_index("mkt")

    loads = [
        pltpu.make_async_copy(source, target, load_sem.at[n])
        for n, (source, target) in enumerate(
            (
                (counts_row_hbm, counts_row_ref),
                (log_share_hbm, log_share_ref),
                (sigma_hbm, sigma_ref),
                (counts_hbm, counts_ref),
                (x_hbm, x_ref),
            )
        )
    ]

    def nu_load(g):
        span = pl.ds(g * group, group)
        return pltpu.make_async_copy(nu_hbm.at[span], nu_ref.at[span], nu_sem.at[g])

    for load in loads:
        load.start()
    for g in range(groups):
        nu_load(g).start()

    barrier = pltpu.get_barrier_semaphore()
    for k in range(1, draws):
        pl.semaphore_signal(
            barrier, inc=1, device_id={"draw": lax.rem(my_draw + k, draws)}, device_id_type=MESH
        )
    for k in range(1, chips):
        pl.semaphore_signal(
            barrier, inc=1, device_id={"mkt": lax.rem(my_mkt + k, chips)}, device_id_type=MESH
        )

    lane = lax.broadcasted_iota(jnp.int32, (slots, LANES), 1)
    row = lax.broadcasted_iota(jnp.int32, (slots, LANES), 0)

    square[...] = jnp.zeros_like(square)
    for load in loads:
        load.wait()
    square[0:markets, 0:slots] = log_share_ref[...]
    log_share = square[...].T[0:slots, :]
    square[0:1, 0:markets] = counts_row_ref[...].astype(jnp.float32)
    counts = square[0:1, :]
    usable = (row.astype(jnp.float32) < counts) & (lane < markets)
    inside = jnp.sum(jnp.where(usable, jnp.exp(log_share), 0.0), axis=0, keepdims=True)
    mean = jnp.where(usable, log_share - jnp.log(1.0 - inside), 0.0)

    coef_row = lax.broadcasted_iota(jnp.int32, (coefs, slots), 0)
    sigma = jnp.zeros((coefs, slots), jnp.float32)
    for k in range(coefs):
        sigma = jnp.where(coef_row == k, sigma_ref[k] * math.log2(math.e), sigma)

    def raised_tastes(m):
        s1, s2 = split2(x_ref[m] * sigma)
        n1, n2 = split2(nu_ref[m])
        left = jnp.concatenate([s1, s1, s2, s2], axis=0).astype(jnp.bfloat16)
        right = jnp.concatenate([n1, n2, n1, n2], axis=0).astype(jnp.bfloat16)
        tastes = lax.dot_general(
            left, right, (((0,), (0,)), ((), ())), preferred_element_type=jnp.float32
        )
        return jnp.exp2(tastes)

    chunks = [
        slice(at, min(at + LANES, nu_ref.shape[2])) for at in range(0, nu_ref.shape[2], LANES)
    ]

    lane8 = lax.broadcasted_iota(jnp.int32, (8, LANES), 1)
    row8 = lax.broadcasted_iota(jnp.int32, (8, LANES), 0)

    def within(tile):
        return (lane8 >= tile * group) & (lane8 < (tile + 1) * group)

    def packed(value, g):
        total = jnp.zeros((8, LANES), jnp.float32)
        for t in range(tiles):
            shift = ((t - g) * group) % LANES
            moved = value[8 * t : 8 * t + 8]
            moved = pltpu.roll(moved, shift, 1) if shift else moved
            total = jnp.where(within(t), moved, total)
        return total

    def unpacked(values):
        rows = []
        for t in range(tiles):
            total = jnp.zeros((8, LANES), jnp.float32)
            for g in range(groups):
                shift = ((g - t) * group) % LANES
                moved = pltpu.roll(values[g], shift, 1) if shift else values[g]
                total = jnp.where(within(g), moved, total)
            rows.append(total)
        return jnp.concatenate(rows, axis=0)

    product = row8
    for t in range(1, tiles):
        product = jnp.where(lane8 >= t * group, row8 + 8 * t, product)
    ls = [packed(log_share, g) for g in range(groups)]
    means = [packed(mean, g) for g in range(groups)]
    wide_counts = jnp.broadcast_to(counts, (slots, LANES))
    valid = [
        (product.astype(jnp.float32) < packed(wide_counts, g)) & (lane8 < tiles * group)
        for g in range(groups)
    ]

    chunks = [
        slice(at, min(at + LANES, nu_ref.shape[2])) for at in range(0, nu_ref.shape[2], LANES)
    ]

    def weight_column(local, i):
        return jnp.concatenate(
            [local[:, t * group + i : t * group + i + 1] for t in range(tiles)], axis=0
        )

    def part_copy(it, k, g):
        return pltpu.make_async_remote_copy(
            src_ref=part_slots.at[it, my_draw, g],
            dst_ref=part_slots.at[it, my_draw, g],
            send_sem=part_send_sem.at[it, k - 1, g],
            recv_sem=part_recv_sem.at[it, k - 1, g],
            device_id={"draw": lax.rem(my_draw + k, draws)},
            device_id_type=MESH,
        )

    def sweep(it):
        def body(g, carry):
            base = g * group
            if it == 0:
                nu_load(g).wait()
            local = weights_ref[g]
            for i in range(group):
                weight = weight_column(local, i)
                known = None
                if it == 0:
                    known = raised_tastes(base + i)
                    held[base + i] = known
                for chunk in chunks:
                    e = held[base + i, :, chunk] if known is None else known[:, chunk]
                    inverse_ref[i : i + 1, chunk] = 1.0 + jnp.sum(
                        weight * e, axis=0, keepdims=True
                    )
            inverse_ref[...] = 1.0 / inverse_ref[...]
            part = jnp.zeros((8, LANES), jnp.float32)
            for i in range(group):
                column = None
                for chunk in chunks:
                    term = held[base + i, :, chunk] * inverse_ref[i : i + 1, chunk]
                    column = term if column is None else column + term
                column = jnp.sum(column, axis=1, keepdims=True)
                for t in range(tiles):
                    part = jnp.where(lane8 == t * group + i, column[8 * t : 8 * t + 8], part)
            part_slots[it, my_draw, g] = part
            if it == 0:

                @pl.when(g == 0)
                def _():
                    pl.semaphore_wait(barrier, draws - 1 + chips - 1)

            for k in range(1, draws):
                part_copy(it, k, g).start()
            return carry

        lax.fori_loop(0, groups, body, 0)

    def peak_copy(it, k):
        return pltpu.make_async_remote_copy(
            src_ref=peak_slots.at[it, 0],
            dst_ref=peak_slots.at[it, k],
            send_sem=peak_send_sem.at[it, k - 1],
            recv_sem=peak_recv_sem.at[it, k - 1],
            device_id={"mkt": lax.rem(my_mkt + k, chips)},
            device_id_type=MESH,
        )

    norms = []
    for it in range(ITERS):
        weights = [jnp.where(valid[g], jnp.exp(means[g]), 0.0) for g in range(groups)]
        for g in range(groups):
            weights_ref[g] = weights[g]
        sweep(it)
        changes = []
        peak = jnp.zeros((8, LANES), jnp.float32)
        for g in range(groups):
            for k in range(1, draws):
                part_copy(it, k, g).wait()
            total = part_slots[it, 0, g]
            for d in range(1, draws):
                total = total + part_slots[it, d, g]
            shares = jnp.where(valid[g], weights[g] * total * inverse, 1.0)
            change = jnp.where(valid[g], ls[g] - jnp.log(shares), 0.0)
            changes.append(change)
            peak = jnp.maximum(peak, jnp.abs(change))
        peak = jnp.max(peak, axis=0, keepdims=True)
        peak = jnp.max(peak, axis=1, keepdims=True)
        peak_slots[it, 0] = jnp.broadcast_to(peak, (1, LANES))
        for k in range(1, chips):
            peak_copy(it, k).start()
        for k in range(1, chips):
            peak_copy(it, k).wait()
        largest = peak_slots[it, 0]
        for k in range(1, chips):
            largest = jnp.maximum(largest, peak_slots[it, k])
        norms.append(largest)
        step = jnp.minimum(1.0, step_cap / (largest + epsilon))
        means = [means[g] + step * changes[g] for g in range(groups)]

    mean = unpacked(means)
    weights = jnp.where(usable, jnp.exp(mean), 0.0)
    ones = jnp.ones((8, nu_ref.shape[2]), jnp.float32)
    cores = 2 if draws % 2 == 0 else 1

    def partner(k):
        chip = (my_draw // cores + (k - 1) // cores + 1) % (draws // cores)
        core = (my_draw + k) % cores
        return chip * cores + core

    def cross_copy(k):
        return pltpu.make_async_remote_copy(
            src_ref=cross_send.at[k - 1],
            dst_ref=cross_slots.at[k - 1],
            send_sem=cross_send_sem.at[k - 1],
            recv_sem=cross_recv_sem.at[k - 1],
            device_id={"draw": partner(k)},
            device_id_type=MESH,
        )

    def last_sweep(k, carry):
        base = partner(k) * own
        local = pltpu.roll(weights, lax.rem(LANES - base, LANES), 1)
        def market(i):
            raised = local[:, i : i + 1] * held[base + i]
            denominator = 1.0 + jnp.sum(raised, axis=0, keepdims=True)
            chance = raised * (1.0 / denominator)
            low = chance - rounded(chance)
            left = jnp.concatenate([chance, low], axis=0).astype(jnp.bfloat16)
            right = jnp.concatenate([chance, ones, low], axis=0).astype(jnp.bfloat16)
            products = lax.dot_general(
                left, right, (((1,), (1,)), ((), ())), preferred_element_type=jnp.float32
            )
            products = jnp.concatenate(
                [products, jnp.zeros((2 * slots, LANES - 2 * slots - 8), jnp.float32)], axis=1
            )
            high = products[0:slots]
            return high + products[slots:] + jnp.where(
                lane < slots, pltpu.roll(high, LANES - slots - 8, 1), 0.0
            )

        def pair_block(first):
            low = market(first)
            if first + 1 < own:
                high = pltpu.roll(market(first + 1), 1, 1)
            else:
                high = low
            return jnp.where(
                lane <= row, low, jnp.where(lane == slots + 2, pltpu.roll(low, 2, 1), high)
            )

        for block in range(cross_send.shape[1]):
            value = pair_block(4 * block)
            if 4 * block + 2 < own:
                value = jnp.where(
                    lane < half, value, pltpu.roll(pair_block(4 * block + 2), half, 1)
                )
            cross_send[k - 1, block] = value

        @pl.when(k < draws)
        def _():
            cross_copy(k).start()

        return carry

    lax.fori_loop(1, draws + 1, last_sweep, 0)

    square[0:slots, :] = mean
    mean_out[...] = square[...].T[0:markets, 0:slots]
    for it in range(ITERS):
        norms_out[it] = norms[it][0, 0]

    for k in range(1, draws):
        cross_copy(k).wait()

    eye = jnp.where(row == lane, 1.0, 0.0)
    for block in range(cross_send.shape[1]):
        total = cross_send[draws - 1, block]
        for k in range(1, draws):
            total = total + cross_slots[k - 1, block]
        square[0:slots, :] = total
        turned_ref[...] = square[...].T
        for i in range(4):
            m = 4 * block + i
            if m >= own:
                continue
            at = (i // 2) * half
            wide = pltpu.roll(total, LANES - at, 1) if at else total
            if i % 2 == 0:
                cross = jnp.where(lane <= row, wide, turned_ref[at : at + slots, :])
                share = wide[:, slots + 2 : slots + 3]
            else:
                cross = jnp.where(
                    lane >= row,
                    pltpu.roll(wide, LANES - 1, 1),
                    turned_ref[at + 1 : at + 1 + slots, :],
                )
                share = wide[:, slots + 1 : slots + 2]
            count = counts_ref[my_draw * own + m]
            here = row < count
            divisor = jnp.where(here[:, 0:1], share, 1.0)
            jac_out[m] = jnp.where(here & (lane < count), eye - cross / divisor, 0.0)[:, 0:slots]


def shards(x_char, nu_draws, coef_sigma, log_share, counts):
    markets, slots, coefs = x_char.shape
    consumers = nu_draws.shape[2]
    draws, chips = lax.axis_size("draw"), lax.axis_size("mkt")
    own = markets // draws
    blocks = -(-own // 4)
    group = divisor_up_to(markets, min(GROUP, LANES // (slots // 8)))
    groups = markets // group
    vmem = pl.BlockSpec(memory_space=pltpu.VMEM)
    smem = pl.BlockSpec(memory_space=pltpu.SMEM)
    f32 = jnp.float32
    return pl.pallas_call(
        functools.partial(kernel, draws, chips, 1.0 / (consumers * draws)),
        out_shape=(
            jax.ShapeDtypeStruct((markets, slots), f32),
            jax.ShapeDtypeStruct((own, slots, slots), f32),
            jax.ShapeDtypeStruct((ITERS,), f32),
        ),
        in_specs=[pl.BlockSpec(memory_space=pltpu.HBM)] * 6,
        out_specs=(vmem, vmem, smem),
        scratch_shapes=[
            pltpu.SMEM((coefs,), f32),
            pltpu.SMEM((markets,), jnp.int32),
            pltpu.VMEM((1, markets), jnp.int32),
            pltpu.VMEM((markets, slots), f32),
            pltpu.VMEM((markets, coefs, slots), f32),
            pltpu.VMEM((markets, coefs, consumers), f32),
            pltpu.VMEM((markets, slots, consumers), f32),
            pltpu.VMEM((group, consumers), f32),
            pltpu.VMEM((groups, 8, LANES), f32),
            pltpu.VMEM((LANES, LANES), f32),
            pltpu.VMEM((LANES, LANES), f32),
            pltpu.VMEM((ITERS, draws, groups, 8, LANES), f32),
            pltpu.VMEM((ITERS, chips, 1, LANES), f32),
            pltpu.VMEM((draws, blocks, slots, LANES), f32),
            pltpu.VMEM((draws, blocks, slots, LANES), f32),
            pltpu.SemaphoreType.DMA((ITERS, draws, groups)),
            pltpu.SemaphoreType.DMA((ITERS, draws, groups)),
            pltpu.SemaphoreType.DMA((ITERS, chips)),
            pltpu.SemaphoreType.DMA((ITERS, chips)),
            pltpu.SemaphoreType.DMA((draws,)),
            pltpu.SemaphoreType.DMA((draws,)),
            pltpu.SemaphoreType.DMA((5,)),
            pltpu.SemaphoreType.DMA((groups,)),
        ],
        compiler_params=pltpu.CompilerParams(
            collective_id=0, has_side_effects=True, vmem_limit_bytes=VMEM_LIMIT
        ),
        name="contraction",
    )(
        coef_sigma,
        counts,
        counts[None, :],
        log_share,
        jnp.swapaxes(x_char, 1, 2),
        nu_draws,
    )


def solution(mesh):
    return jax.shard_map(
        shards,
        mesh=mesh,
        in_specs=(P("mkt", None, None), P("mkt", None, "draw"), P(), P("mkt", None), P("mkt")),
        out_specs=(P("mkt", None), P(("mkt", "draw"), None, None), P()),
        check_vma=False,
    )
```

```python
import functools
import math

import jax
import jax.numpy as jnp
from jax import lax
from jax.experimental import pallas as pl
from jax.experimental.pallas import tpu as pltpu
from jax.sharding import PartitionSpec as P

ITERS = 3
LANES = 128
GROUP = 16
VMEM_LIMIT = 48 * 1024 * 1024
MESH = pl.DeviceIdType.MESH

step_cap = 0.25
epsilon = 1e-06


def divisor_up_to(count, most):
    return max(size for size in range(1, most + 1) if count % size == 0)


def rounded(value):
    return value.astype(jnp.bfloat16).astype(jnp.float32)


def split2(value):
    first = rounded(value)
    return first, value - first


def kernel(
    draws,
    chips,
    inverse,
    sigma_hbm,
    counts_hbm,
    counts_row_hbm,
    log_share_hbm,
    x_hbm,
    nu_hbm,
    mean_out,
    jac_out,
    norms_out,
    sigma_ref,
    counts_ref,
    counts_row_ref,
    log_share_ref,
    x_ref,
    nu_ref,
    held,
    inverse_ref,
    weights_ref,
    turned_ref,
    square,
    part_slots,
    peak_slots,
    cross_send,
    cross_slots,
    part_send_sem,
    part_recv_sem,
    peak_send_sem,
    peak_recv_sem,
    cross_send_sem,
    cross_recv_sem,
    load_sem,
    nu_sem,
):
    markets, coefs, slots = x_ref.shape
    own = markets // draws
    half = LANES // 2
    tiles = slots // 8
    group = divisor_up_to(markets, min(GROUP, LANES // tiles))
    groups = markets // group
    my_draw = lax.axis_index("draw")
    my_mkt = lax.axis_index("mkt")

    loads = [
        pltpu.make_async_copy(source, target, load_sem.at[n])
        for n, (source, target) in enumerate(
            (
                (counts_row_hbm, counts_row_ref),
                (log_share_hbm, log_share_ref),
                (sigma_hbm, sigma_ref),
                (counts_hbm, counts_ref),
                (x_hbm, x_ref),
            )
        )
    ]

    def nu_load(g):
        span = pl.ds(g * group, group)
        return pltpu.make_async_copy(nu_hbm.at[span], nu_ref.at[span], nu_sem.at[g])

    for load in loads:
        load.start()
    for g in range(groups):
        nu_load(g).start()

    barrier = pltpu.get_barrier_semaphore()
    for k in range(1, draws):
        pl.semaphore_signal(
            barrier, inc=1, device_id={"draw": lax.rem(my_draw + k, draws)}, device_id_type=MESH
        )
    for k in range(1, chips):
        pl.semaphore_signal(
            barrier, inc=1, device_id={"mkt": lax.rem(my_mkt + k, chips)}, device_id_type=MESH
        )

    lane = lax.broadcasted_iota(jnp.int32, (slots, LANES), 1)
    row = lax.broadcasted_iota(jnp.int32, (slots, LANES), 0)

    square[...] = jnp.zeros_like(square)
    for load in loads:
        load.wait()
    square[0:markets, 0:slots] = log_share_ref[...]
    log_share = square[...].T[0:slots, :]
    square[0:1, 0:markets] = counts_row_ref[...].astype(jnp.float32)
    counts = square[0:1, :]
    usable = (row.astype(jnp.float32) < counts) & (lane < markets)
    inside = jnp.sum(jnp.where(usable, jnp.exp(log_share), 0.0), axis=0, keepdims=True)
    mean = jnp.where(usable, log_share - jnp.log(1.0 - inside), 0.0)

    coef_row = lax.broadcasted_iota(jnp.int32, (coefs, slots), 0)
    sigma = jnp.zeros((coefs, slots), jnp.float32)
    for k in range(coefs):
        sigma = jnp.where(coef_row == k, sigma_ref[k] * math.log2(math.e), sigma)

    def raised_tastes(m):
        s1, s2 = split2(x_ref[m] * sigma)
        n1, n2 = split2(nu_ref[m])
        left = jnp.concatenate([s1, s1, s2, s2], axis=0).astype(jnp.bfloat16)
        right = jnp.concatenate([n1, n2, n1, n2], axis=0).astype(jnp.bfloat16)
        tastes = lax.dot_general(
            left, right, (((0,), (0,)), ((), ())), preferred_element_type=jnp.float32
        )
        return jnp.exp2(tastes)

    chunks = [
        slice(at, min(at + LANES, nu_ref.shape[2])) for at in range(0, nu_ref.shape[2], LANES)
    ]

    lane8 = lax.broadcasted_iota(jnp.int32, (8, LANES), 1)
    row8 = lax.broadcasted_iota(jnp.int32, (8, LANES), 0)

    def within(tile):
        return (lane8 >= tile * group) & (lane8 < (tile + 1) * group)

    def packed(value, g):
        total = jnp.zeros((8, LANES), jnp.float32)
        for t in range(tiles):
            shift = ((t - g) * group) % LANES
            moved = value[8 * t : 8 * t + 8]
            moved = pltpu.roll(moved, shift, 1) if shift else moved
            total = jnp.where(within(t), moved, total)
        return total

    def unpacked(values):
        rows = []
        for t in range(tiles):
            total = jnp.zeros((8, LANES), jnp.float32)
            for g in range(groups):
                shift = ((g - t) * group) % LANES
                moved = pltpu.roll(values[g], shift, 1) if shift else values[g]
                total = jnp.where(within(g), moved, total)
            rows.append(total)
        return jnp.concatenate(rows, axis=0)

    product = row8
    for t in range(1, tiles):
        product = jnp.where(lane8 >= t * group, row8 + 8 * t, product)
    ls = [packed(log_share, g) for g in range(groups)]
    means = [packed(mean, g) for g in range(groups)]
    wide_counts = jnp.broadcast_to(counts, (slots, LANES))
    valid = [
        (product.astype(jnp.float32) < packed(wide_counts, g)) & (lane8 < tiles * group)
        for g in range(groups)
    ]

    chunks = [
        slice(at, min(at + LANES, nu_ref.shape[2])) for at in range(0, nu_ref.shape[2], LANES)
    ]

    def weight_column(local, i):
        return jnp.concatenate(
            [local[:, t * group + i : t * group + i + 1] for t in range(tiles)], axis=0
        )

    def part_copy(it, k, g):
        return pltpu.make_async_remote_copy(
            src_ref=part_slots.at[it, my_draw, g],
            dst_ref=part_slots.at[it, my_draw, g],
            send_sem=part_send_sem.at[it, k - 1, g],
            recv_sem=part_recv_sem.at[it, k - 1, g],
            device_id={"draw": lax.rem(my_draw + k, draws)},
            device_id_type=MESH,
        )

    def sweep(it):
        def body(g, carry):
            base = g * group
            if it == 0:
                nu_load(g).wait()
            local = weights_ref[g]
            for i in range(group):
                weight = weight_column(local, i)
                known = None
                if it == 0:
                    known = raised_tastes(base + i)
                    held[base + i] = known
                for chunk in chunks:
                    e = held[base + i, :, chunk] if known is None else known[:, chunk]
                    inverse_ref[i : i + 1, chunk] = 1.0 + jnp.sum(
                        weight * e, axis=0, keepdims=True
                    )
            inverse_ref[...] = 1.0 / inverse_ref[...]
            part = jnp.zeros((8, LANES), jnp.float32)
            for i in range(group):
                column = None
                for chunk in chunks:
                    term = held[base + i, :, chunk] * inverse_ref[i : i + 1, chunk]
                    column = term if column is None else column + term
                column = jnp.sum(column, axis=1, keepdims=True)
                for t in range(tiles):
                    part = jnp.where(lane8 == t * group + i, column[8 * t : 8 * t + 8], part)
            part_slots[it, my_draw, g] = part
            if it == 0:

                @pl.when(g == 0)
                def _():
                    pl.semaphore_wait(barrier, draws - 1 + chips - 1)

            for k in range(1, draws):
                part_copy(it, k, g).start()
            return carry

        lax.fori_loop(0, groups, body, 0)

    def peak_copy(it, k):
        return pltpu.make_async_remote_copy(
            src_ref=peak_slots.at[it, 0],
            dst_ref=peak_slots.at[it, k],
            send_sem=peak_send_sem.at[it, k - 1],
            recv_sem=peak_recv_sem.at[it, k - 1],
            device_id={"mkt": lax.rem(my_mkt + k, chips)},
            device_id_type=MESH,
        )

    norms = []
    for it in range(ITERS):
        weights = [jnp.where(valid[g], jnp.exp(means[g]), 0.0) for g in range(groups)]
        for g in range(groups):
            weights_ref[g] = weights[g]
        sweep(it)
        changes = []
        peak = jnp.zeros((8, LANES), jnp.float32)
        for g in range(groups):
            for k in range(1, draws):
                part_copy(it, k, g).wait()
            total = part_slots[it, 0, g]
            for d in range(1, draws):
                total = total + part_slots[it, d, g]
            shares = jnp.where(valid[g], weights[g] * total * inverse, 1.0)
            change = jnp.where(valid[g], ls[g] - jnp.log(shares), 0.0)
            changes.append(change)
            peak = jnp.maximum(peak, jnp.abs(change))
        peak = jnp.max(peak, axis=0, keepdims=True)
        peak = jnp.max(peak, axis=1, keepdims=True)
        peak_slots[it, 0] = jnp.broadcast_to(peak, (1, LANES))
        for k in range(1, chips):
            peak_copy(it, k).start()
        for k in range(1, chips):
            peak_copy(it, k).wait()
        largest = peak_slots[it, 0]
        for k in range(1, chips):
            largest = jnp.maximum(largest, peak_slots[it, k])
        norms.append(largest)
        step = jnp.minimum(1.0, step_cap / (largest + epsilon))
        means = [means[g] + step * changes[g] for g in range(groups)]

    mean = unpacked(means)
    weights = jnp.where(usable, jnp.exp(mean), 0.0)
    ones = jnp.ones((8, nu_ref.shape[2]), jnp.float32)
    cores = 2 if draws % 2 == 0 else 1

    def partner(k):
        chip = (my_draw // cores + (k - 1) // cores + 1) % (draws // cores)
        core = (my_draw + k) % cores
        return chip * cores + core

    def cross_copy(k):
        return pltpu.make_async_remote_copy(
            src_ref=cross_send.at[k - 1],
            dst_ref=cross_slots.at[k - 1],
            send_sem=cross_send_sem.at[k - 1],
            recv_sem=cross_recv_sem.at[k - 1],
            device_id={"draw": partner(k)},
            device_id_type=MESH,
        )

    def last_sweep(k, carry):
        base = partner(k) * own
        local = pltpu.roll(weights, lax.rem(LANES - base, LANES), 1)
        def market(i):
            raised = local[:, i : i + 1] * held[base + i]
            denominator = 1.0 + jnp.sum(raised, axis=0, keepdims=True)
            chance = raised * (1.0 / denominator)
            low = chance - rounded(chance)
            left = jnp.concatenate([chance, low], axis=0).astype(jnp.bfloat16)
            right = jnp.concatenate([chance, ones, low], axis=0).astype(jnp.bfloat16)
            products = lax.dot_general(
                left, right, (((1,), (1,)), ((), ())), preferred_element_type=jnp.float32
            )
            products = jnp.concatenate(
                [products, jnp.zeros((2 * slots, LANES - 2 * slots - 8), jnp.float32)], axis=1
            )
            high = products[0:slots]
            return high + products[slots:] + jnp.where(
                lane < slots, pltpu.roll(high, LANES - slots - 8, 1), 0.0
            )

        def pair_block(first):
            low = market(first)
            if first + 1 < own:
                high = pltpu.roll(market(first + 1), 1, 1)
            else:
                high = low
            return jnp.where(
                lane <= row, low, jnp.where(lane == slots + 2, pltpu.roll(low, 2, 1), high)
            )

        for block in range(cross_send.shape[1]):
            value = pair_block(4 * block)
            if 4 * block + 2 < own:
                value = jnp.where(
                    lane < half, value, pltpu.roll(pair_block(4 * block + 2), half, 1)
                )
            cross_send[k - 1, block] = value

        @pl.when(k < draws)
        def _():
            cross_copy(k).start()

        return carry

    lax.fori_loop(1, draws + 1, last_sweep, 0)

    square[0:slots, :] = mean
    mean_out[...] = square[...].T[0:markets, 0:slots]
    for it in range(ITERS):
        norms_out[it] = norms[it][0, 0]

    for k in range(1, draws):
        cross_copy(k).wait()

    eye = jnp.where(row == lane, 1.0, 0.0)
    for block in range(cross_send.shape[1]):
        total = cross_send[draws - 1, block]
        for k in range(1, draws):
            total = total + cross_slots[k - 1, block]
        square[0:slots, :] = total
        turned_ref[...] = square[...].T
        for i in range(4):
            m = 4 * block + i
            if m >= own:
                continue
            at = (i // 2) * half
            wide = pltpu.roll(total, LANES - at, 1) if at else total
            if i % 2 == 0:
                cross = jnp.where(lane <= row, wide, turned_ref[at : at + slots, :])
                share = wide[:, slots + 2 : slots + 3]
            else:
                cross = jnp.where(
                    lane >= row,
                    pltpu.roll(wide, LANES - 1, 1),
                    turned_ref[at + 1 : at + 1 + slots, :],
                )
                share = wide[:, slots + 1 : slots + 2]
            count = counts_ref[my_draw * own + m]
            here = row < count
            divisor = jnp.where(here[:, 0:1], share, 1.0)
            jac_out[m] = jnp.where(here & (lane < count), eye - cross * (1.0 / divisor), 0.0)[:, 0:slots]


def shards(x_char, nu_draws, coef_sigma, log_share, counts):
    markets, slots, coefs = x_char.shape
    consumers = nu_draws.shape[2]
    draws, chips = lax.axis_size("draw"), lax.axis_size("mkt")
    own = markets // draws
    blocks = -(-own // 4)
    group = divisor_up_to(markets, min(GROUP, LANES // (slots // 8)))
    groups = markets // group
    vmem = pl.BlockSpec(memory_space=pltpu.VMEM)
    smem = pl.BlockSpec(memory_space=pltpu.SMEM)
    f32 = jnp.float32
    return pl.pallas_call(
        functools.partial(kernel, draws, chips, 1.0 / (consumers * draws)),
        out_shape=(
            jax.ShapeDtypeStruct((markets, slots), f32),
            jax.ShapeDtypeStruct((own, slots, slots), f32),
            jax.ShapeDtypeStruct((ITERS,), f32),
        ),
        in_specs=[pl.BlockSpec(memory_space=pltpu.HBM)] * 6,
        out_specs=(vmem, vmem, smem),
        scratch_shapes=[
            pltpu.SMEM((coefs,), f32),
            pltpu.SMEM((markets,), jnp.int32),
            pltpu.VMEM((1, markets), jnp.int32),
            pltpu.VMEM((markets, slots), f32),
            pltpu.VMEM((markets, coefs, slots), f32),
            pltpu.VMEM((markets, coefs, consumers), f32),
            pltpu.VMEM((markets, slots, consumers), f32),
            pltpu.VMEM((group, consumers), f32),
            pltpu.VMEM((groups, 8, LANES), f32),
            pltpu.VMEM((LANES, LANES), f32),
            pltpu.VMEM((LANES, LANES), f32),
            pltpu.VMEM((ITERS, draws, groups, 8, LANES), f32),
            pltpu.VMEM((ITERS, chips, 1, LANES), f32),
            pltpu.VMEM((draws, blocks, slots, LANES), f32),
            pltpu.VMEM((draws, blocks, slots, LANES), f32),
            pltpu.SemaphoreType.DMA((ITERS, draws, groups)),
            pltpu.SemaphoreType.DMA((ITERS, draws, groups)),
            pltpu.SemaphoreType.DMA((ITERS, chips)),
            pltpu.SemaphoreType.DMA((ITERS, chips)),
            pltpu.SemaphoreType.DMA((draws,)),
            pltpu.SemaphoreType.DMA((draws,)),
            pltpu.SemaphoreType.DMA((5,)),
            pltpu.SemaphoreType.DMA((groups,)),
        ],
        compiler_params=pltpu.CompilerParams(
            collective_id=0, has_side_effects=True, vmem_limit_bytes=VMEM_LIMIT
        ),
        name="contraction",
    )(
        *(
            pltpu.with_memory_space_constraint(operand, pltpu.HBM)
            for operand in (
                coef_sigma,
                counts,
                counts[None, :],
                log_share,
                jnp.swapaxes(x_char, 1, 2),
                nu_draws,
            )
        )
    )


def solution(mesh):
    return jax.shard_map(
        shards,
        mesh=mesh,
        in_specs=(P("mkt", None, None), P("mkt", None, "draw"), P(), P("mkt", None), P("mkt")),
        out_specs=(P("mkt", None), P(("mkt", "draw"), None, None), P()),
        check_vma=False,
    )
```

```python
import functools
import math

import jax
import jax.numpy as jnp
from jax import lax
from jax.experimental import pallas as pl
from jax.experimental.pallas import tpu as pltpu
from jax.sharding import PartitionSpec as P

ITERS = 3
LANES = 128
GROUP = 16
VMEM_LIMIT = 48 * 1024 * 1024
MESH = pl.DeviceIdType.MESH

step_cap = 0.25
epsilon = 1e-06


def divisor_up_to(count, most):
    return max(size for size in range(1, most + 1) if count % size == 0)


def rounded(value):
    return value.astype(jnp.bfloat16).astype(jnp.float32)


def split2(value):
    first = rounded(value)
    return first, value - first


def kernel(
    draws,
    chips,
    inverse,
    sigma_hbm,
    counts_hbm,
    counts_row_hbm,
    log_share_hbm,
    x_hbm,
    nu_hbm,
    mean_out,
    jac_out,
    norms_out,
    sigma_ref,
    counts_ref,
    counts_row_ref,
    log_share_ref,
    x_ref,
    nu_ref,
    held,
    inverse_ref,
    weights_ref,
    turned_ref,
    square,
    part_slots,
    peak_slots,
    cross_send,
    cross_slots,
    part_send_sem,
    part_recv_sem,
    peak_send_sem,
    peak_recv_sem,
    cross_send_sem,
    cross_recv_sem,
    load_sem,
    nu_sem,
):
    markets, coefs, slots = x_ref.shape
    own = markets // draws
    half = LANES // 2
    tiles = slots // 8
    group = divisor_up_to(markets, min(GROUP, LANES // tiles))
    groups = markets // group
    my_draw = lax.axis_index("draw")
    my_mkt = lax.axis_index("mkt")

    loads = [
        pltpu.make_async_copy(source, target, load_sem.at[n])
        for n, (source, target) in enumerate(
            (
                (counts_row_hbm, counts_row_ref),
                (log_share_hbm, log_share_ref),
                (sigma_hbm, sigma_ref),
                (counts_hbm, counts_ref),
                (x_hbm, x_ref),
            )
        )
    ]

    def nu_load(g):
        span = pl.ds(g * group, group)
        return pltpu.make_async_copy(nu_hbm.at[span], nu_ref.at[span], nu_sem.at[g])

    for load in loads:
        load.start()
    for g in range(groups):
        nu_load(g).start()

    barrier = pltpu.get_barrier_semaphore()
    for k in range(1, draws):
        pl.semaphore_signal(
            barrier, inc=1, device_id={"draw": lax.rem(my_draw + k, draws)}, device_id_type=MESH
        )
    for k in range(1, chips):
        pl.semaphore_signal(
            barrier, inc=1, device_id={"mkt": lax.rem(my_mkt + k, chips)}, device_id_type=MESH
        )

    lane = lax.broadcasted_iota(jnp.int32, (slots, LANES), 1)
    row = lax.broadcasted_iota(jnp.int32, (slots, LANES), 0)

    square[...] = jnp.zeros_like(square)
    for load in loads:
        load.wait()
    square[0:markets, 0:slots] = log_share_ref[...]
    log_share = square[...].T[0:slots, :]
    square[0:1, 0:markets] = counts_row_ref[...].astype(jnp.float32)
    counts = square[0:1, :]
    usable = (row.astype(jnp.float32) < counts) & (lane < markets)
    inside = jnp.sum(jnp.where(usable, jnp.exp(log_share), 0.0), axis=0, keepdims=True)
    mean = jnp.where(usable, log_share - jnp.log(1.0 - inside), 0.0)

    coef_row = lax.broadcasted_iota(jnp.int32, (coefs, slots), 0)
    sigma = jnp.zeros((coefs, slots), jnp.float32)
    for k in range(coefs):
        sigma = jnp.where(coef_row == k, sigma_ref[k] * math.log2(math.e), sigma)

    def raised_tastes(m):
        s1, s2 = split2(x_ref[m] * sigma)
        n1, n2 = split2(nu_ref[m])
        left = jnp.concatenate([s1, s1, s2, s2], axis=0).astype(jnp.bfloat16)
        right = jnp.concatenate([n1, n2, n1, n2], axis=0).astype(jnp.bfloat16)
        tastes = lax.dot_general(
            left, right, (((0,), (0,)), ((), ())), preferred_element_type=jnp.float32
        )
        return jnp.exp2(tastes)

    chunks = [
        slice(at, min(at + LANES, nu_ref.shape[2])) for at in range(0, nu_ref.shape[2], LANES)
    ]

    lane8 = lax.broadcasted_iota(jnp.int32, (8, LANES), 1)
    row8 = lax.broadcasted_iota(jnp.int32, (8, LANES), 0)

    def within(tile):
        return (lane8 >= tile * group) & (lane8 < (tile + 1) * group)

    def packed(value, g):
        total = jnp.zeros((8, LANES), jnp.float32)
        for t in range(tiles):
            shift = ((t - g) * group) % LANES
            moved = value[8 * t : 8 * t + 8]
            moved = pltpu.roll(moved, shift, 1) if shift else moved
            total = jnp.where(within(t), moved, total)
        return total

    def unpacked(values):
        rows = []
        for t in range(tiles):
            total = jnp.zeros((8, LANES), jnp.float32)
            for g in range(groups):
                shift = ((g - t) * group) % LANES
                moved = pltpu.roll(values[g], shift, 1) if shift else values[g]
                total = jnp.where(within(g), moved, total)
            rows.append(total)
        return jnp.concatenate(rows, axis=0)

    product = row8
    for t in range(1, tiles):
        product = jnp.where(lane8 >= t * group, row8 + 8 * t, product)
    ls = [packed(log_share, g) for g in range(groups)]
    means = [packed(mean, g) for g in range(groups)]
    wide_counts = jnp.broadcast_to(counts, (slots, LANES))
    valid = [
        (product.astype(jnp.float32) < packed(wide_counts, g)) & (lane8 < tiles * group)
        for g in range(groups)
    ]

    chunks = [
        slice(at, min(at + LANES, nu_ref.shape[2])) for at in range(0, nu_ref.shape[2], LANES)
    ]

    def weight_column(local, i):
        return jnp.concatenate(
            [local[:, t * group + i : t * group + i + 1] for t in range(tiles)], axis=0
        )

    def part_copy(it, k, g):
        return pltpu.make_async_remote_copy(
            src_ref=part_slots.at[it, my_draw, g],
            dst_ref=part_slots.at[it, my_draw, g],
            send_sem=part_send_sem.at[it, k - 1, g],
            recv_sem=part_recv_sem.at[it, k - 1, g],
            device_id={"draw": lax.rem(my_draw + k, draws)},
            device_id_type=MESH,
        )

    def sweep(it):
        def body(g, carry):
            base = g * group
            if it == 0:
                nu_load(g).wait()
            local = weights_ref[g]
            for i in range(group):
                weight = weight_column(local, i)
                known = None
                if it == 0:
                    known = raised_tastes(base + i)
                    held[base + i] = known
                for chunk in chunks:
                    e = held[base + i, :, chunk] if known is None else known[:, chunk]
                    inverse_ref[i : i + 1, chunk] = 1.0 + jnp.sum(
                        weight * e, axis=0, keepdims=True
                    )
            inverse_ref[...] = 1.0 / inverse_ref[...]
            part = jnp.zeros((8, LANES), jnp.float32)
            for i in range(group):
                column = None
                for chunk in chunks:
                    term = held[base + i, :, chunk] * inverse_ref[i : i + 1, chunk]
                    column = term if column is None else column + term
                column = jnp.sum(column, axis=1, keepdims=True)
                for t in range(tiles):
                    part = jnp.where(lane8 == t * group + i, column[8 * t : 8 * t + 8], part)
            part_slots[it, my_draw, g] = part
            if it == 0:

                @pl.when(g == 0)
                def _():
                    pl.semaphore_wait(barrier, draws - 1 + chips - 1)

            for k in range(1, draws):
                part_copy(it, k, g).start()
            return carry

        lax.fori_loop(0, groups, body, 0)

    def peak_copy(it, k):
        return pltpu.make_async_remote_copy(
            src_ref=peak_slots.at[it, 0],
            dst_ref=peak_slots.at[it, k],
            send_sem=peak_send_sem.at[it, k - 1],
            recv_sem=peak_recv_sem.at[it, k - 1],
            device_id={"mkt": lax.rem(my_mkt + k, chips)},
            device_id_type=MESH,
        )

    norms = []
    for it in range(ITERS):
        weights = [jnp.where(valid[g], jnp.exp(means[g]), 0.0) for g in range(groups)]
        for g in range(groups):
            weights_ref[g] = weights[g]
        sweep(it)
        changes = []
        peak = jnp.zeros((8, LANES), jnp.float32)
        for g in range(groups):
            for k in range(1, draws):
                part_copy(it, k, g).wait_recv()
            total = part_slots[it, 0, g]
            for d in range(1, draws):
                total = total + part_slots[it, d, g]
            shares = jnp.where(valid[g], weights[g] * total * inverse, 1.0)
            change = jnp.where(valid[g], ls[g] - jnp.log(shares), 0.0)
            changes.append(change)
            peak = jnp.maximum(peak, jnp.abs(change))
        peak = jnp.max(peak, axis=0, keepdims=True)
        peak = jnp.max(peak, axis=1, keepdims=True)
        peak_slots[it, 0] = jnp.broadcast_to(peak, (1, LANES))
        for k in sorted(range(1, chips), key=lambda k: -min(k, chips - k)):
            peak_copy(it, k).start()
        for k in range(1, chips):
            peak_copy(it, k).wait_recv()
        largest = peak_slots[it, 0]
        for k in range(1, chips):
            largest = jnp.maximum(largest, peak_slots[it, k])
        norms.append(largest)
        step = jnp.minimum(1.0, step_cap / (largest + epsilon))
        means = [means[g] + step * changes[g] for g in range(groups)]

    mean = unpacked(means)
    weights = jnp.where(usable, jnp.exp(mean), 0.0)
    ones = jnp.ones((8, nu_ref.shape[2]), jnp.float32)
    cores = 2 if draws % 2 == 0 else 1

    def partner(k):
        chip = (my_draw // cores + (k - 1) // cores + 1) % (draws // cores)
        core = (my_draw + k) % cores
        return chip * cores + core

    def cross_copy(k):
        return pltpu.make_async_remote_copy(
            src_ref=cross_send.at[k - 1],
            dst_ref=cross_slots.at[k - 1],
            send_sem=cross_send_sem.at[k - 1],
            recv_sem=cross_recv_sem.at[k - 1],
            device_id={"draw": partner(k)},
            device_id_type=MESH,
        )

    def last_sweep(k, carry):
        base = partner(k) * own
        local = pltpu.roll(weights, lax.rem(LANES - base, LANES), 1)
        def market(i):
            raised = local[:, i : i + 1] * held[base + i]
            denominator = 1.0 + jnp.sum(raised, axis=0, keepdims=True)
            chance = raised * (1.0 / denominator)
            low = chance - rounded(chance)
            left = jnp.concatenate([chance, low], axis=0).astype(jnp.bfloat16)
            right = jnp.concatenate([chance, ones, low], axis=0).astype(jnp.bfloat16)
            products = lax.dot_general(
                left, right, (((1,), (1,)), ((), ())), preferred_element_type=jnp.float32
            )
            products = jnp.concatenate(
                [products, jnp.zeros((2 * slots, LANES - 2 * slots - 8), jnp.float32)], axis=1
            )
            high = products[0:slots]
            return high + products[slots:] + jnp.where(
                lane < slots, pltpu.roll(high, LANES - slots - 8, 1), 0.0
            )

        def pair_block(first):
            low = market(first)
            if first + 1 < own:
                high = pltpu.roll(market(first + 1), 1, 1)
            else:
                high = low
            return jnp.where(
                lane <= row, low, jnp.where(lane == slots + 2, pltpu.roll(low, 2, 1), high)
            )

        for block in range(cross_send.shape[1]):
            value = pair_block(4 * block)
            if 4 * block + 2 < own:
                value = jnp.where(
                    lane < half, value, pltpu.roll(pair_block(4 * block + 2), half, 1)
                )
            cross_send[k - 1, block] = value

        @pl.when(k < draws)
        def _():
            cross_copy(k).start()

        return carry

    lax.fori_loop(1, draws + 1, last_sweep, 0)

    square[0:slots, :] = mean
    mean_out[...] = square[...].T[0:markets, 0:slots]
    for it in range(ITERS):
        norms_out[it] = norms[it][0, 0]

    for it in range(ITERS):
        for k in range(1, chips):
            peak_copy(it, k).wait_send()
        for k in range(1, draws):
            for g in range(groups):
                part_copy(it, k, g).wait_send()
    for k in range(1, draws):
        cross_copy(k).wait()

    eye = jnp.where(row == lane, 1.0, 0.0)
    for block in range(cross_send.shape[1]):
        total = cross_send[draws - 1, block]
        for k in range(1, draws):
            total = total + cross_slots[k - 1, block]
        square[0:slots, :] = total
        turned_ref[...] = square[...].T
        for i in range(4):
            m = 4 * block + i
            if m >= own:
                continue
            at = (i // 2) * half
            wide = pltpu.roll(total, LANES - at, 1) if at else total
            if i % 2 == 0:
                cross = jnp.where(lane <= row, wide, turned_ref[at : at + slots, :])
                share = wide[:, slots + 2 : slots + 3]
            else:
                cross = jnp.where(
                    lane >= row,
                    pltpu.roll(wide, LANES - 1, 1),
                    turned_ref[at + 1 : at + 1 + slots, :],
                )
                share = wide[:, slots + 1 : slots + 2]
            count = counts_ref[my_draw * own + m]
            here = row < count
            divisor = jnp.where(here[:, 0:1], share, 1.0)
            jac_out[m] = jnp.where(here & (lane < count), eye - cross * (1.0 / divisor), 0.0)[:, 0:slots]


def shards(x_char, nu_draws, coef_sigma, log_share, counts):
    markets, slots, coefs = x_char.shape
    consumers = nu_draws.shape[2]
    draws, chips = lax.axis_size("draw"), lax.axis_size("mkt")
    own = markets // draws
    blocks = -(-own // 4)
    group = divisor_up_to(markets, min(GROUP, LANES // (slots // 8)))
    groups = markets // group
    vmem = pl.BlockSpec(memory_space=pltpu.VMEM)
    smem = pl.BlockSpec(memory_space=pltpu.SMEM)
    f32 = jnp.float32
    return pl.pallas_call(
        functools.partial(kernel, draws, chips, 1.0 / (consumers * draws)),
        out_shape=(
            jax.ShapeDtypeStruct((markets, slots), f32),
            jax.ShapeDtypeStruct((own, slots, slots), f32),
            jax.ShapeDtypeStruct((ITERS,), f32),
        ),
        in_specs=[pl.BlockSpec(memory_space=pltpu.HBM)] * 6,
        out_specs=(vmem, vmem, smem),
        scratch_shapes=[
            pltpu.SMEM((coefs,), f32),
            pltpu.SMEM((markets,), jnp.int32),
            pltpu.VMEM((1, markets), jnp.int32),
            pltpu.VMEM((markets, slots), f32),
            pltpu.VMEM((markets, coefs, slots), f32),
            pltpu.VMEM((markets, coefs, consumers), f32),
            pltpu.VMEM((markets, slots, consumers), f32),
            pltpu.VMEM((group, consumers), f32),
            pltpu.VMEM((groups, 8, LANES), f32),
            pltpu.VMEM((LANES, LANES), f32),
            pltpu.VMEM((LANES, LANES), f32),
            pltpu.VMEM((ITERS, draws, groups, 8, LANES), f32),
            pltpu.VMEM((ITERS, chips, 1, LANES), f32),
            pltpu.VMEM((draws, blocks, slots, LANES), f32),
            pltpu.VMEM((draws, blocks, slots, LANES), f32),
            pltpu.SemaphoreType.DMA((ITERS, draws, groups)),
            pltpu.SemaphoreType.DMA((ITERS, draws, groups)),
            pltpu.SemaphoreType.DMA((ITERS, chips)),
            pltpu.SemaphoreType.DMA((ITERS, chips)),
            pltpu.SemaphoreType.DMA((draws,)),
            pltpu.SemaphoreType.DMA((draws,)),
            pltpu.SemaphoreType.DMA((5,)),
            pltpu.SemaphoreType.DMA((groups,)),
        ],
        compiler_params=pltpu.CompilerParams(
            collective_id=0, has_side_effects=True, vmem_limit_bytes=VMEM_LIMIT
        ),
        name="contraction",
    )(
        *(
            pltpu.with_memory_space_constraint(operand, pltpu.HBM)
            for operand in (
                coef_sigma,
                counts,
                counts[None, :],
                log_share,
                jnp.swapaxes(x_char, 1, 2),
                nu_draws,
            )
        )
    )


def solution(mesh):
    return jax.shard_map(
        shards,
        mesh=mesh,
        in_specs=(P("mkt", None, None), P("mkt", None, "draw"), P(), P("mkt", None), P("mkt")),
        out_specs=(P("mkt", None), P(("mkt", "draw"), None, None), P()),
        check_vma=False,
    )
```
